32 devices in a mesh: fsdp: 4 (over y, core), ctx: 2 (over x), tensor: 4 (over z).
Axes of the slice: x: 2, y: 2, z: 4, core: 2. Of those that a mesh axis runs over, the one named last changes fastest.
Arguments:
- inputs: bfloat16 [4, 2048, 2048], P('fsdp', ('ctx', 'tensor')), may hold values from -6 to 6
- prefix: int32 [4], P('fsdp'), may hold values from 204 to 1024
- query_weight: bfloat16 [2048, 2048], P(('fsdp', 'ctx'), 'tensor'), may hold values from -0.125 to 0.125
- key_weight: bfloat16 [2048, 2048], P(('fsdp', 'ctx'), 'tensor'), may hold values from -0.125 to 0.125
- value_weight: bfloat16 [2048, 2048], P(('fsdp', 'ctx'), 'tensor'), may hold values from -0.125 to 0.125
- out_weight: bfloat16 [2048, 2048], P('tensor', ('fsdp', 'ctx')), may hold values from -0.125 to 0.125
- gate_weight: bfloat16 [2048, 8192], P(('fsdp', 'ctx'), 'tensor'), may hold values from -0.125 to 0.125
- up_weight: bfloat16 [2048, 8192], P(('fsdp', 'ctx'), 'tensor'), may hold values from -0.125 to 0.125
- down_weight: bfloat16 [8192, 2048], P('tensor', ('fsdp', 'ctx')), may hold values from -0.0625 to 0.0625
- query_gain: float32 [2048], P(('fsdp', 'ctx', 'tensor')), may hold values from 0.25 to 1.75
- key_gain: float32 [2048], P(('fsdp', 'ctx', 'tensor')), may hold values from 0.25 to 1.75
- attn_gain: float32 [2048], P(('fsdp', 'ctx', 'tensor')), may hold values from 0.25 to 1.75
- ff_gain: float32 [2048], P(('fsdp', 'ctx', 'tensor')), may hold values from 0.25 to 1.75
- cotangent: bfloat16 [4, 2048, 2048], P('fsdp', ('ctx', 'tensor')), may hold values from -6 to 6
Outputs:
- output: bfloat16 [4, 2048, 2048], P('fsdp', ('ctx', 'tensor'))
- inputs_grad: float32 [4, 2048, 2048], P('fsdp', ('ctx', 'tensor'))
- query_weight_grad: float32 [2048, 2048], P(('fsdp', 'ctx'), 'tensor')
- key_weight_grad: float32 [2048, 2048], P(('fsdp', 'ctx'), 'tensor')
- value_weight_grad: float32 [2048, 2048], P(('fsdp', 'ctx'), 'tensor')
- out_weight_grad: float32 [2048, 2048], P('tensor', ('fsdp', 'ctx'))
- gate_weight_grad: float32 [2048, 8192], P(('fsdp', 'ctx'), 'tensor')
- up_weight_grad: float32 [2048, 8192], P(('fsdp', 'ctx'), 'tensor')
- down_weight_grad: float32 [8192, 2048], P('tensor', ('fsdp', 'ctx'))
- query_gain_grad: float32 [2048], P(('fsdp', 'ctx', 'tensor'))
- key_gain_grad: float32 [2048], P(('fsdp', 'ctx', 'tensor'))
- attn_gain_grad: float32 [2048], P(('fsdp', 'ctx', 'tensor'))
- ff_gain_grad: float32 [2048], P(('fsdp', 'ctx', 'tensor'))
The draws below stay inside these ranges and needn't reach their ends.
All inputs are finite; a program needn't handle non-finite values.
Results may differ from the reference program's by a relative error of at most 0.02.
Values may be sent and summed in bfloat16 or wider, within the bound.
No kernel may reach another device: no remote copies, remote signals or barrier semaphores. Data moves between devices by JAX's collectives and lax.ppermute only.
A program may use at most 256 MiB of HBM per device.

```python
import math
import jax
import jax.numpy as jnp
from jax import lax

D = 2048
HEADS = 16
HEAD_DIM = 128
FF = 8192
LEN = 2048
SEQS = 4


def set_ends(result, stream_key, low, high):
    longest = result.shape.index(max(result.shape))
    spots = []
    for shift in (0, 1):
        where = [jax.random.randint(jax.random.fold_in(stream_key, axis), (), 0, length) for axis, length in enumerate(result.shape)]
        where[longest] = (where[longest] + shift) % result.shape[longest]
        spots.append(tuple(where))
    return result.at[spots[0]].set(low).at[spots[1]].set(high)


def levels(own_key, shape, shards, smallest, high):
    def one(dim, shards_of):
        draws = jax.random.uniform(jax.random.fold_in(jax.random.fold_in(own_key, 6), dim), (shards_of,), jnp.float32, smallest / len(shards), high / len(shards))
        return jnp.repeat(jnp.exp(draws), shape[dim] // shards_of).reshape((-1,) + (1,) * (len(shape) - dim - 1))

    gain = one(*shards[0])
    for cut in shards[1:]:
        gain = gain * one(*cut)
    return gain


def bell_draw(rng, shape, width, reach, shards=(), held_as=jnp.bfloat16):
    result = width * jax.random.normal(rng, shape, jnp.float32)
    if shards:
        result = result * levels(rng, shape, shards, -0.22, 0.18)
    return jnp.clip(result, -reach, reach).astype(held_as)


def setup_inputs(seed: int = 0) -> dict:
    seeds = jax.random.split(jax.random.key(seed), 15)
    return {
        "inputs": bell_draw(seeds[0], (SEQS, LEN, D), 1.0, 6.0, ((0, 4), (1, 8))),
        "prefix": set_ends(jax.random.randint(seeds[1], (SEQS,), LEN // 10, LEN // 2 + 1), jax.random.fold_in(seeds[1], 1), LEN // 10, (LEN // 2 + 1) - 1).astype(jnp.int32),
        "query_weight": bell_draw(seeds[2], (D, D), D ** -0.5, 0.125, ((0, 8), (1, 4))),
        "key_weight": bell_draw(seeds[3], (D, D), D ** -0.5, 0.125, ((0, 8), (1, 4))),
        "value_weight": bell_draw(seeds[4], (D, D), D ** -0.5, 0.125, ((0, 8), (1, 4))),
        "out_weight": bell_draw(seeds[5], (D, D), D ** -0.5, 0.125, ((0, 4), (1, 8))),
        "gate_weight": bell_draw(seeds[6], (D, FF), D ** -0.5, 0.125, ((0, 8), (1, 4))),
        "up_weight": bell_draw(seeds[7], (D, FF), D ** -0.5, 0.125, ((0, 8), (1, 4))),
        "down_weight": bell_draw(seeds[8], (FF, D), FF ** -0.5, 0.0625, ((0, 4), (1, 8))),
        "query_gain": jnp.clip(1.0 + 0.15 * jax.random.normal(seeds[9], (D,), jnp.float32), 0.25, 1.75),
        "key_gain": jnp.clip(1.0 + 0.15 * jax.random.normal(seeds[10], (D,), jnp.float32), 0.25, 1.75),
        "attn_gain": jnp.clip(1.0 + 0.15 * jax.random.normal(seeds[11], (D,), jnp.float32), 0.25, 1.75),
        "ff_gain": jnp.clip(1.0 + 0.15 * jax.random.normal(seeds[12], (D,), jnp.float32), 0.25, 1.75),
        "cotangent": bell_draw(seeds[13], (SEQS, LEN, D), 1.0, 6.0, ((0, 4), (1, 8))),
    }


EPS = 1e-06
THETA = 500000.0
MASKED = -1e+30

@jax.custom_vjp
def low(v):
    return lax.optimization_barrier(v.astype(jnp.bfloat16)).astype(jnp.float32)

@jax.custom_vjp
def low_back(v):
    return v

def low_keep(v):
    return (low(v), None)

def low_pass(kept, grad):
    return (grad,)

def back_keep(v):
    return (v, None)

def back_low(kept, grad):
    return (low(grad),)
low.defvjp(low_keep, low_pass)
low_back.defvjp(back_keep, back_low)

def product(left, right):
    return jnp.dot(left, right, precision=lax.Precision.HIGHEST)

def inverse_rms(values):
    return lax.rsqrt(lax.optimization_barrier(jnp.mean(values * values, axis=-1, keepdims=True)) + EPS)

def rotate(values, cosines, sines):
    half_dim = values.shape[-1] // 2
    leading = values[..., :half_dim]
    trailing = values[..., half_dim:]
    cos_part = cosines[:, None, :]
    sin_part = sines[:, None, :]
    return jnp.concatenate([leading * cos_part - trailing * sin_part, trailing * cos_part + leading * sin_part], axis=-1)

def one_sequence(tokens, prefix_end, weights):
    w_query, w_key, w_value, w_out, w_gate, w_up, w_down, gain_query, gain_key, gain_attn, gain_ff = weights
    length = tokens.shape[0]
    half_dim = HEAD_DIM // 2
    frequency = THETA ** (-(jnp.arange(half_dim, dtype=jnp.float32) * 2.0 / HEAD_DIM))
    angles = jnp.arange(length, dtype=jnp.float32)[:, None] * frequency[None, :]
    cosines = jnp.cos(angles)
    sines = jnp.sin(angles)
    head_shape = (length, HEADS, HEAD_DIM)
    query_raw = low_back(product(tokens, w_query))
    key_raw = low_back(product(tokens, w_key))
    value_raw = low_back(product(tokens, w_value))
    queries = low(rotate((query_raw * inverse_rms(query_raw) * gain_query).reshape(head_shape), cosines, sines))
    keys = low(rotate((key_raw * inverse_rms(key_raw) * gain_key).reshape(head_shape), cosines, sines))
    values = low(value_raw).reshape(head_shape)
    scores = low_back(jnp.einsum('qhd,khd->hqk', queries, keys, precision=lax.Precision.HIGHEST) / math.sqrt(HEAD_DIM))
    row_ids = jnp.arange(length)[:, None]
    col_ids = jnp.arange(length)[None, :]
    allowed = ((col_ids <= row_ids) | (col_ids < prefix_end))[None]
    masked = jnp.where(allowed, scores, MASKED)
    row_peak = lax.optimization_barrier(jnp.max(masked, axis=-1, keepdims=True))
    log_total = row_peak + jnp.log(lax.optimization_barrier(jnp.sum(jnp.exp(masked - row_peak), axis=-1, keepdims=True)))
    probs = low(jnp.exp(masked - log_total))
    mixture = jnp.einsum('hqk,khd->qhd', probs, values, precision=lax.Precision.HIGHEST)
    attended = low(low_back(mixture)).reshape(length, HEADS * HEAD_DIM)
    branch_attn = low_back(product(attended, w_out))
    hidden_state = tokens + branch_attn * inverse_rms(branch_attn) * gain_attn
    hidden_low = low(hidden_state)
    gate = low_back(product(hidden_low, w_gate))
    up_proj = low_back(product(hidden_low, w_up))
    inner = low(jax.nn.silu(gate) * up_proj)
    branch_ff = low_back(product(inner, w_down))
    return low(hidden_state + branch_ff * inverse_rms(branch_ff) * gain_ff)

def reference(inputs, prefix, query_weight, key_weight, value_weight, out_weight, gate_weight, up_weight, down_weight, query_gain, key_gain, attn_gain, ff_gain, cotangent):
    floats = [operand.astype(jnp.float32) for operand in (inputs, query_weight, key_weight, value_weight, out_weight, gate_weight, up_weight, down_weight, query_gain, key_gain, attn_gain, ff_gain)]

    def forward(tokens_all, *weights):

        def per_sequence(paired):
            return one_sequence(paired[0], paired[1], weights)
        return lax.map(jax.checkpoint(per_sequence), (tokens_all, prefix))
    output, pullback = jax.vjp(forward, *floats)
    grads = pullback(cotangent.astype(jnp.float32))
    return (output.astype(jnp.bfloat16), grads[0], grads[1], grads[2], grads[3], grads[4], grads[5], grads[6], grads[7], grads[8], grads[9], grads[10], grads[11])
```

```python
import functools
import math

import jax
import jax.numpy as jnp
from jax import lax
from jax.experimental import pallas as pl
from jax.experimental.pallas import tpu as pltpu
from jax.sharding import PartitionSpec as P

HEAD_DIM = 128
EPS = 1e-06
THETA = 500000.0
MASKED = -1e30
LOG2E = math.log2(math.e)
F32 = jnp.float32
BF16 = jnp.bfloat16


NT = (((1,), (1,)), ((), ()))
TN = (((0,), (0,)), ((), ()))


def dot(a, b, dims=(((1,), (0,)), ((), ()))):
    return lax.dot_general(a, b, dims, preferred_element_type=F32)


def place(info_ref, a, n):
    return lax.rem(info_ref[0] - a + n, n)


def allowed_mask(kv_start, q_start, prefix, rows):
    kv = kv_start + lax.broadcasted_iota(jnp.int32, (rows, rows), 0)
    q = q_start + lax.broadcasted_iota(jnp.int32, (rows, rows), 1)
    return (kv <= q) | (kv < prefix)


def forward_kernel(
    info_ref, q_ref, kl_ref, vl_ref, kr_ref, vr_ref, o_ref, lse_ref, m_ref, l_ref, acc_ref, *, n, heads, rows
):
    part, prefix = info_ref[1], info_ref[2]
    factor = LOG2E / math.sqrt(HEAD_DIM)

    def update(row, col, k_ref, v_ref, mask):
        for h in range(heads):
            lanes = slice(h * HEAD_DIM, (h + 1) * HEAD_DIM)
            q = q_ref[pl.ds(row, rows), lanes]
            k = k_ref[pl.ds(col, rows), lanes]
            v = v_ref[pl.ds(col, rows), lanes]
            s = dot(k, q, NT)
            if mask is not None:
                s = jnp.where(mask, s, MASKED)
            m_old = m_ref[h : h + 1]
            m_new = jnp.maximum(m_old, jnp.max(s, axis=0, keepdims=True))
            p = jnp.exp2((s - m_new) * factor)
            alpha = jnp.exp2((m_old - m_new) * factor)
            m_ref[h : h + 1] = m_new
            l_ref[h : h + 1] = alpha * l_ref[h : h + 1] + jnp.sum(p, axis=0, keepdims=True)
            acc_ref[lanes] = alpha * acc_ref[lanes] + dot(v, p.astype(BF16), TN)

    def block(aq, carry):
        spot = place(info_ref, aq, n)
        row = pl.multiple_of(spot * rows, rows)
        m_ref[...] = jnp.full_like(m_ref, MASKED)
        l_ref[...] = jnp.zeros_like(l_ref)
        acc_ref[...] = jnp.zeros_like(acc_ref)

        def remote(b, c):
            update(row, pl.multiple_of(b * rows, rows), kr_ref, vr_ref, None)
            return c

        lax.fori_loop(0, jnp.where(part == 1, n, 0), remote, 0)

        def full(a, c):
            update(row, pl.multiple_of(place(info_ref, a, n) * rows, rows), kl_ref, vl_ref, None)
            return c

        lax.fori_loop(0, aq, full, 0)

        def masked(a, c):
            mask = allowed_mask(a * rows, aq * rows, jnp.where(part == 0, prefix, 0), rows)
            update(row, pl.multiple_of(place(info_ref, a, n) * rows, rows), kl_ref, vl_ref, mask)
            return c

        top = jnp.where(part == 0, jnp.minimum((prefix + rows - 1) // rows, n), 0)
        lax.fori_loop(aq, jnp.maximum(top, aq + 1), masked, 0)
        for h in range(heads):
            lanes = slice(h * HEAD_DIM, (h + 1) * HEAD_DIM)
            total = l_ref[h : h + 1]
            mix = acc_ref[lanes] / total
            o_ref[pl.ds(row, rows), lanes] = mix.T.astype(BF16)
            lse_ref[spot, h : h + 1] = m_ref[h : h + 1] * factor + jnp.log2(total)
        return carry

    lax.fori_loop(0, n, block, 0)


def pair_back(q, k, v, do, lse, delta, mask, factor):
    s = dot(k, q, NT)
    p = jnp.exp2(s * factor - lse)
    if mask is not None:
        p = jnp.where(mask, p, 0.0)
    dp = dot(v, do, NT)
    ds = (p * (dp - delta)).astype(BF16)
    return dot(p.astype(BF16), do), dot(ds, q), dot(ds, k, TN)


def deltas(do_ref, o_ref, delta_ref, n, heads, rows):
    for b in range(n):
        for h in range(heads):
            lanes = slice(h * HEAD_DIM, (h + 1) * HEAD_DIM)
            span = slice(b * rows, (b + 1) * rows)
            t = do_ref[span, lanes].astype(F32) * o_ref[span, lanes].astype(F32)
            delta_ref[b, h : h + 1] = jnp.sum(t.T, axis=0, keepdims=True)


def remote_back_kernel(
    info_ref, q_ref, k_ref, v_ref, do_ref, o_ref, lse_ref,
    dq_ref, dk_ref, dv_ref, delta_ref, dk_acc, dv_acc, *, n, heads, rows,
):
    factor = LOG2E / math.sqrt(HEAD_DIM)
    root = 1.0 / math.sqrt(HEAD_DIM)
    dq_ref[...] = jnp.zeros_like(dq_ref)

    @pl.when(info_ref[1] == 1)
    def _():
        deltas(do_ref, o_ref, delta_ref, n, heads, rows)

        def kv_block(b, carry):
            col = pl.multiple_of(b * rows, rows)
            dk_acc[...] = jnp.zeros_like(dk_acc)
            dv_acc[...] = jnp.zeros_like(dv_acc)

            def q_block(spot, c):
                row = pl.multiple_of(spot * rows, rows)
                for h in range(heads):
                    lanes = slice(h * HEAD_DIM, (h + 1) * HEAD_DIM)
                    dv, dk, dq = pair_back(
                        q_ref[pl.ds(row, rows), lanes], k_ref[pl.ds(col, rows), lanes],
                        v_ref[pl.ds(col, rows), lanes], do_ref[pl.ds(row, rows), lanes],
                        lse_ref[spot, h : h + 1], delta_ref[spot, h : h + 1], None, factor,
                    )
                    dv_acc[:, lanes] += dv
                    dk_acc[:, lanes] += dk
                    dq_ref[pl.ds(row, rows), lanes] += dq
                return c

            lax.fori_loop(0, n, q_block, 0)
            dk_ref[pl.ds(col, rows)] = (dk_acc[...] * root).astype(BF16)
            dv_ref[pl.ds(col, rows)] = dv_acc[...].astype(BF16)
            return carry

        lax.fori_loop(0, n, kv_block, 0)


def local_back_kernel(
    info_ref, q_ref, k_ref, v_ref, do_ref, o_ref, lse_ref, dq_in_ref,
    dq_ref, dk_ref, dv_ref, delta_ref, *, n, heads, rows,
):
    part, prefix = info_ref[1], info_ref[2]
    factor = LOG2E / math.sqrt(HEAD_DIM)
    root = 1.0 / math.sqrt(HEAD_DIM)
    deltas(do_ref, o_ref, delta_ref, n, heads, rows)
    dq_ref[...] = dq_in_ref[...]
    dk_ref[...] = jnp.zeros_like(dk_ref)
    dv_ref[...] = jnp.zeros_like(dv_ref)

    def pair(aq, col, mask):
        spot = place(info_ref, aq, n)
        row = pl.multiple_of(spot * rows, rows)
        for h in range(heads):
            lanes = slice(h * HEAD_DIM, (h + 1) * HEAD_DIM)
            dv, dk, dq = pair_back(
                q_ref[pl.ds(row, rows), lanes], k_ref[pl.ds(col, rows), lanes],
                v_ref[pl.ds(col, rows), lanes], do_ref[pl.ds(row, rows), lanes],
                lse_ref[spot, h : h + 1], delta_ref[spot, h : h + 1], mask, factor,
            )
            dv_ref[pl.ds(col, rows), lanes] += dv
            dk_ref[pl.ds(col, rows), lanes] += dk
            dq_ref[pl.ds(row, rows), lanes] += dq

    def kv_block(a, carry):
        col = pl.multiple_of(place(info_ref, a, n) * rows, rows)

        def masked(aq, c):
            pair(aq, col, allowed_mask(a * rows, aq * rows, jnp.where(part == 0, prefix, 0), rows))
            return c

        low = jnp.where((part == 0) & (a * rows < prefix), 0, a)
        lax.fori_loop(low, a + 1, masked, 0)

        def full(aq, c):
            pair(aq, col, None)
            return c

        lax.fori_loop(a + 1, n, full, 0)
        return carry

    lax.fori_loop(0, n, kv_block, 0)
    dq_ref[...] = dq_ref[...] * root
    dk_ref[...] = dk_ref[...] * root


def columns_of(total_ref, b, width):
    return lax.rsqrt(total_ref[b] / width + EPS).T


def turned(values):
    return pltpu.roll(values, HEAD_DIM // 2, 1)


def rope_kernel(total_ref, gains_ref, cos_ref, sin_ref, *refs, n, heads, rows, width):
    raws, (q_ref, k_ref) = refs[:n], refs[n:]
    half = heads * HEAD_DIM
    for b in range(n):
        scales = columns_of(total_ref, b, width)
        span = slice(b * rows, (b + 1) * rows)
        cos, sin = cos_ref[span], sin_ref[span]
        for which, out in ((0, q_ref), (1, k_ref)):
            scale = scales[:, which : which + 1]
            for h in range(heads):
                lanes = slice(h * HEAD_DIM, (h + 1) * HEAD_DIM)
                raw = raws[b][:, which * half + h * HEAD_DIM : which * half + (h + 1) * HEAD_DIM]
                normed = raw * scale * gains_ref[which : which + 1, lanes]
                out[span, lanes] = (normed * cos + turned(normed) * sin).astype(BF16)


def unrope_kernel(
    total_ref, gains_ref, cos_ref, sin_ref, dq_ref, dk_ref, dkr_ref, *refs, n, heads, rows, width
):
    raws, (dots_ref, gain_ref, dqn_ref, dkn_ref) = refs[:n], refs[n:]
    half = heads * HEAD_DIM
    receives = dkr_ref is not None
    gain_ref[...] = jnp.zeros_like(gain_ref)
    for b in range(n):
        scales = columns_of(total_ref, b, width)
        span = slice(b * rows, (b + 1) * rows)
        cos, sin = cos_ref[span], sin_ref[span]
        sums = []
        for which, out in ((0, dqn_ref), (1, dkn_ref)):
            scale = scales[:, which : which + 1]
            row_term = None
            for h in range(heads):
                lanes = slice(h * HEAD_DIM, (h + 1) * HEAD_DIM)
                if which == 0:
                    grad = dq_ref[span, lanes]
                else:
                    grad = dk_ref[span, lanes] + dkr_ref[span, lanes].astype(F32)
                grad = grad * cos - turned(grad) * sin
                raw = raws[b][:, which * half + h * HEAD_DIM : which * half + (h + 1) * HEAD_DIM]
                weighted = grad * gains_ref[which : which + 1, lanes]
                out[span, lanes] = weighted
                product = grad * raw
                gain_ref[which : which + 1, lanes] += jnp.sum(product * scale, axis=0, keepdims=True)
                term = weighted * raw
                row_term = term if row_term is None else row_term + term
            sums.append(jnp.sum(row_term.T, axis=0, keepdims=True))
        dots_ref[b] = jnp.concatenate(sums + [jnp.zeros((6, rows), F32)], axis=0)


def raw_back_kernel(total_ref, dots_ref, dqn_ref, dkn_ref, dv_ref, dvr_ref, *refs, n, heads, rows, width):
    raws, (out_ref,) = refs[:n], refs[n:]
    half = heads * HEAD_DIM
    for b in range(n):
        scales = columns_of(total_ref, b, width)
        dots = (dots_ref[b] / width).T
        span = slice(b * rows, (b + 1) * rows)
        for which, grad_ref in ((0, dqn_ref), (1, dkn_ref)):
            scale = scales[:, which : which + 1]
            factor = scale * scale * scale * dots[:, which : which + 1]
            raw = raws[b][:, which * half : (which + 1) * half]
            out_ref[span, which * half : (which + 1) * half] = (
                grad_ref[span] * scale - raw * factor
            ).astype(BF16)
        out_ref[span, 2 * half :] = (dv_ref[span] + dvr_ref[span].astype(F32)).astype(BF16)


def call(kernel, name, outs, args, scratch=(), flops=0, scalars=0, limit=60 << 20, aliases=None):
    moved = sum(a.size * a.dtype.itemsize for a in args) + sum(
        o.size * o.dtype.itemsize for o in outs
    )
    spec = pl.BlockSpec(memory_space=pltpu.VMEM)
    specs = [pl.BlockSpec(memory_space=pltpu.SMEM)] * scalars + [spec] * (len(args) - scalars)
    return pl.pallas_call(
        kernel,
        out_shape=tuple(outs),
        in_specs=specs,
        out_specs=tuple(spec for _ in outs),
        scratch_shapes=list(scratch),
        compiler_params=pltpu.CompilerParams(vmem_limit_bytes=limit),
        cost_estimate=pl.CostEstimate(flops=flops, transcendentals=flops // 512, bytes_accessed=moved),
        name=name,
    )(*args)


def ring(n):
    return [(i, (i + 1) % n) for i in range(n)]


def gather_ring(block, n):
    blocks = [block]
    for _ in range(n - 1):
        blocks.append(lax.ppermute(blocks[-1], "tensor", ring(n)))
    return blocks


def scatter_ring(term, n):
    moving = term(1).astype(BF16)
    for k in range(2, n + 1):
        moving = lax.ppermute(moving, "tensor", ring(n))
        total = moving.astype(F32) + term(k % n)
        moving = total.astype(BF16)
    return total


def block_sums(values, n):
    total = values
    for shift in range(1, n):
        there = lax.ppermute(values, "tensor", [(i, (i + shift) % n) for i in range(n)])
        total = total + jnp.concatenate([there[n - shift :], there[: n - shift]], axis=0)
    return total


def all_sum(values, sizes):
    for axis, size in sizes:
        step = 1
        while step < size:
            values = values + lax.ppermute(values, axis, [(i, i ^ step) for i in range(size)])
            step *= 2
    return values


def fetch(shard, axis):
    return lax.all_gather(shard, ("fsdp", "ctx"), axis=axis, tiled=True)


def hand_in(grad, axis):
    return lax.psum_scatter(grad, ("fsdp", "ctx"), scatter_dimension=axis, tiled=True)


def inverse_rms(values, width):
    return lax.rsqrt(jnp.sum(values * values, axis=-1, keepdims=True) / width + EPS)


def norm_back(values, scale, weighted, total, width):
    return scale * weighted - values * scale * scale * scale * (total / width)


def on_device(
    sizes,
    inputs,
    prefix,
    query_weight,
    key_weight,
    value_weight,
    out_weight,
    gate_weight,
    up_weight,
    down_weight,
    query_gain,
    key_gain,
    attn_gain,
    ff_gain,
    cotangent,
):
    seqs, rows, width = inputs.shape
    n = dict(sizes)["tensor"]
    if seqs != 1 or dict(sizes)["ctx"] != 2:
        raise ValueError("sizes")
    z = lax.axis_index("tensor")
    part = lax.axis_index("ctx")
    local_width = query_weight.shape[1]
    heads = local_width // HEAD_DIM
    hidden = gate_weight.shape[1]
    group = n * rows
    gain_rows = query_gain.shape[0]
    own = (lax.axis_index("fsdp") * 2 + part) * n + z
    column_start = z * local_width

    x = inputs[0]
    w_qkv = fetch(jnp.concatenate([query_weight, key_weight, value_weight], axis=1), 0)
    w_out = fetch(out_weight, 1)
    w_gu = fetch(jnp.concatenate([gate_weight, up_weight], axis=1), 0)
    w_down = fetch(down_weight, 1)

    gains_own = jnp.stack([query_gain, key_gain, attn_gain, ff_gain])
    gains = all_sum(
        lax.dynamic_update_slice(jnp.zeros((4, width), F32), gains_own, (0, own * gain_rows)), sizes
    )
    gain_attn, gain_ff = gains[2], gains[3]
    gains_qk = lax.dynamic_slice(gains, (0, column_start), (2, local_width))

    info = jnp.stack([z, part, prefix[0]]).astype(jnp.int32)

    half_dim = HEAD_DIM // 2
    frequency = THETA ** (-(jnp.arange(half_dim, dtype=F32) * 2.0 / HEAD_DIM))
    starts = part * group + lax.rem(z - jnp.arange(n) + n, n) * rows
    positions = (starts[:, None] + jnp.arange(rows)[None, :]).reshape(group)
    angles = positions.astype(F32)[:, None] * frequency[None, :]
    cosines, sines = jnp.cos(angles), jnp.sin(angles)
    cos_all = jnp.concatenate([cosines, cosines], axis=1)
    sin_all = jnp.concatenate([-sines, sines], axis=1)

    xs = gather_ring(x, n)
    raws = [dot(b, w_qkv) for b in xs]
    v_local = jnp.concatenate([r[:, 2 * local_width :].astype(BF16) for r in raws], axis=0)
    raws = [r[:, : 2 * local_width] for r in raws]
    squares = jnp.stack(
        [
            jnp.concatenate(
                [
                    jnp.sum(jnp.square(r.reshape(rows, 2, local_width)), axis=-1).T,
                    jnp.zeros((6, rows), F32),
                ],
                axis=0,
            )
            for r in raws
        ]
    )
    totals = block_sums(squares, n)
    block_shape = jax.ShapeDtypeStruct((group, local_width), BF16)
    wide_shape = jax.ShapeDtypeStruct((group, local_width), F32)
    row_shape = jax.ShapeDtypeStruct((n, 8, rows), F32)
    static = dict(n=n, heads=heads, rows=rows)
    q, k_local = call(
        functools.partial(rope_kernel, width=width, **static),
        "rope",
        (block_shape, block_shape),
        (totals, gains_qk, cos_all, sin_all, *raws),
        flops=40 * group * local_width,
    )
    to_second = [(0, 1)]
    k_remote = lax.ppermute(k_local, "ctx", to_second)
    v_remote = lax.ppermute(v_local, "ctx", to_second)
    pairs = 2 * group * group * local_width
    attended, lse = call(
        functools.partial(forward_kernel, **static),
        "attend",
        (block_shape, row_shape),
        (info, q, k_local, v_local, k_remote, v_remote),
        scratch=(
            pltpu.VMEM((8, rows), F32),
            pltpu.VMEM((8, rows), F32),
            pltpu.VMEM((local_width, rows), F32),
        ),
        flops=4 * pairs,
        scalars=1,
    )
    branch_attn = scatter_ring(lambda k: dot(attended[k * rows : (k + 1) * rows], w_out), n)
    attn_scale = inverse_rms(branch_attn, width)
    hidden_state = x.astype(F32) + branch_attn * attn_scale * gain_attn

    hs = gather_ring(hidden_state.astype(BF16), n)
    gus = [dot(b, w_gu) for b in hs]
    sigs = [jax.nn.sigmoid(g[:, :hidden]) for g in gus]
    inners = [(g[:, :hidden] * s * g[:, hidden:]).astype(BF16) for g, s in zip(gus, sigs)]
    branch_ff = scatter_ring(lambda k: dot(inners[k], w_down), n)
    ff_scale = inverse_rms(branch_ff, width)
    output = (hidden_state + branch_ff * ff_scale * gain_ff).astype(BF16)

    upstream = cotangent[0].astype(F32)
    ff_weighted = gain_ff * upstream
    ff_gain_term = jnp.sum(upstream * branch_ff * ff_scale, axis=0)
    d_branch_ff = norm_back(
        branch_ff, ff_scale, ff_weighted, jnp.sum(ff_weighted * branch_ff, axis=-1, keepdims=True), width
    )
    es = gather_ring(d_branch_ff.astype(BF16), n)
    d_gus = []
    for e, g, s in zip(es, gus, sigs):
        gate, up = g[:, :hidden], g[:, hidden:]
        d_inner = dot(e, w_down, NT)
        d_gate = (d_inner * up * s * (1.0 + gate * (1.0 - s))).astype(BF16)
        d_up = (d_inner * gate * s).astype(BF16)
        d_gus.append(jnp.concatenate([d_gate, d_up], axis=1))
    d_hidden = upstream + scatter_ring(lambda k: dot(d_gus[k], w_gu, NT), n)
    e_all = jnp.concatenate(es, axis=0)
    down_grad = hand_in(dot(jnp.concatenate(inners, axis=0), e_all, TN).astype(BF16), 1)
    gu_grad = hand_in(
        dot(jnp.concatenate(hs, axis=0), jnp.concatenate(d_gus, axis=0), TN).astype(BF16), 0
    )

    attn_weighted = gain_attn * d_hidden
    attn_gain_term = jnp.sum(d_hidden * branch_attn * attn_scale, axis=0)
    d_branch_attn = norm_back(
        branch_attn,
        attn_scale,
        attn_weighted,
        jnp.sum(attn_weighted * branch_attn, axis=-1, keepdims=True),
        width,
    )
    d_attn = gather_ring(d_branch_attn.astype(BF16), n)
    d_attended = jnp.concatenate([dot(b, w_out, NT).astype(BF16) for b in d_attn], axis=0)
    out_grad = hand_in(dot(attended, jnp.concatenate(d_attn, axis=0), TN).astype(BF16), 1)
    delta_scratch = pltpu.VMEM((n, 8, rows), F32)
    dq_remote, dk_remote, dv_remote = call(
        functools.partial(remote_back_kernel, **static),
        "remote_back",
        (wide_shape, block_shape, block_shape),
        (info, q, k_remote, v_remote, d_attended, attended, lse),
        scratch=(delta_scratch, pltpu.VMEM((rows, local_width), F32), pltpu.VMEM((rows, local_width), F32)),
        flops=5 * pairs,
        scalars=1,
    )
    to_first = [(1, 0)]
    dk_sent = lax.ppermute(dk_remote, "ctx", to_first)
    dv_sent = lax.ppermute(dv_remote, "ctx", to_first)
    dq, dk, dv = call(
        functools.partial(local_back_kernel, **static),
        "local_back",
        (wide_shape, wide_shape, wide_shape),
        (info, q, k_local, v_local, d_attended, attended, lse, dq_remote),
        scratch=(delta_scratch,),
        flops=3 * pairs,
        scalars=1,
    )
    dots, qk_gain_term, dqn, dkn = call(
        functools.partial(unrope_kernel, width=width, **static),
        "unrope",
        (row_shape, jax.ShapeDtypeStruct((8, local_width), F32), wide_shape, wide_shape),
        (totals, gains_qk, cos_all, sin_all, dq, dk, dk_sent, *raws),
        flops=40 * group * local_width,
    )
    dot_totals = block_sums(dots, n)
    (d_raw,) = call(
        functools.partial(raw_back_kernel, width=width, **static),
        "raw_back",
        (jax.ShapeDtypeStruct((group, 3 * local_width), BF16),),
        (totals, dot_totals, dqn, dkn, dv, dv_sent, *raws),
        flops=40 * group * local_width,
    )
    inputs_grad = d_hidden + scatter_ring(lambda k: dot(d_raw[k * rows : (k + 1) * rows], w_qkv, NT), n)
    qkv_grad = hand_in(dot(jnp.concatenate(xs, axis=0), d_raw, TN).astype(BF16), 0)

    gain_terms = jnp.concatenate(
        [
            lax.dynamic_update_slice(jnp.zeros((2, width), F32), qk_gain_term[:2], (0, column_start)),
            attn_gain_term[None],
            ff_gain_term[None],
        ],
        axis=0,
    )
    gain_grads = lax.dynamic_slice(all_sum(gain_terms, sizes), (0, own * gain_rows), (4, gain_rows))
    qkv_grad = qkv_grad.astype(F32)
    gu_grad = gu_grad.astype(F32)
    return (
        output[None],
        inputs_grad[None],
        qkv_grad[:, :local_width],
        qkv_grad[:, local_width : 2 * local_width],
        qkv_grad[:, 2 * local_width :],
        out_grad.astype(F32),
        gu_grad[:, :hidden],
        gu_grad[:, hidden:],
        down_grad.astype(F32),
        gain_grads[0],
        gain_grads[1],
        gain_grads[2],
        gain_grads[3],
    )


def solution(mesh):
    tokens = P("fsdp", ("ctx", "tensor"), None)
    columns = P(("fsdp", "ctx"), "tensor")
    rows = P("tensor", ("fsdp", "ctx"))
    gain = P(("fsdp", "ctx", "tensor"))
    in_specs = (
        tokens, P("fsdp"), columns, columns, columns, rows, columns, columns, rows,
        gain, gain, gain, gain, tokens,
    )
    out_specs = (
        tokens, tokens, columns, columns, columns, rows, columns, columns, rows, gain, gain, gain, gain,
    )
    sizes = tuple((axis, mesh.shape[axis]) for axis in ("fsdp", "ctx", "tensor"))
    return jax.shard_map(
        functools.partial(on_device, sizes),
        mesh=mesh, in_specs=in_specs, out_specs=out_specs, check_vma=False,
    )
```
